256 devices in a mesh: blk: 16 (over x, z_lo, core), grp: 16 (over z_hi, y).
Axes of the slice: x: 4, y: 4, z: 8 (z_hi: 4, z_lo: 2; z = z_hi * 2 + z_lo), core: 2. Of those that a mesh axis runs over, the one named last changes fastest.
Arguments:
- amplitudes: bfloat16 [12288, 1024], P(('blk', 'grp')), may hold values from -6 to 6
- integrals: bfloat16 [1024, 65536], P(None, ('grp', 'blk')), may hold values from -0.1875 to 0.1875
- amplitude_mask: int32 [768, 8], P(('blk', 'grp')), may hold values 0 or 1
- integral_mask: int32 [8, 512], P(None, ('grp', 'blk')), may hold values 0 or 1
Outputs:
- residual: bfloat16 [12288, 65536], P('blk', 'grp')
The draws below stay inside these ranges and needn't reach their ends.
All inputs are finite; a program needn't handle non-finite values. No bound on the sum of `amplitude_mask` or of `integral_mask` on one device may be relied on, other than what follows from the above.
Results may differ from the reference program's by a relative error of at most 0.001.
Values may be sent and summed in bfloat16 or wider, within the bound.
A program may use at most 64 MiB of HBM per device.

```python
import jax
import jax.numpy as jnp
from jax import lax

TILE = 128
OTILE = 16
CD_TILES = 8
CD = 1024
OP = 12288
AB = 65536
N_BLK = 16


def set_ends(values, stream_key, low, top_value):
    shape = values.shape
    index_at = [jax.random.randint(jax.random.fold_in(stream_key, axis), (), 0, shape[axis]) for axis in range(len(shape))]
    values = values.at[tuple(index_at)].set(low)
    longest = shape.index(max(shape))
    index_at[longest] = (index_at[longest] + 1) % shape[longest]
    return values.at[tuple(index_at)].set(top_value)


def levels(stream_key, extent, split, least, largest):
    def one(axis_at, parts):
        draws = jax.random.uniform(jax.random.fold_in(jax.random.fold_in(stream_key, 6), axis_at), (parts,), jnp.float32, least / len(split), largest / len(split))
        return jnp.repeat(jnp.exp(draws), extent[axis_at] // parts).reshape((-1,) + (1,) * (len(extent) - axis_at - 1))

    gain = one(*split[0])
    for cut in split[1:]:
        gain = gain * one(*cut)
    return gain


def gaussian(key, dims, scale, reach, cuts=(), kind=jnp.bfloat16):
    factor_of = levels(key, dims, cuts, -0.22, 0.18) if cuts else 1.0
    entries = jax.random.normal(key, dims, jnp.float32) * scale * factor_of
    return jnp.minimum(jnp.maximum(entries, -reach), reach).astype(kind)


def setup_inputs(seed: int = 0) -> dict:
    key_list = jax.random.split(jax.random.key(seed), 5)
    amplitudes = gaussian(key_list[0], (OP, CD), 1.0, 6.0, ((0, 256),))
    integrals = gaussian(key_list[1], (CD, AB), CD ** -0.5, 0.1875, ((1, 256),))
    amplitude_mask = set_ends((jax.random.randint(key_list[2], (OP // OTILE, CD_TILES), 0, 4) < 3).astype(jnp.int32), jax.random.fold_in(key_list[2], 1), 0, 1)
    integral_mask = set_ends((jax.random.randint(key_list[3], (CD_TILES, AB // TILE), 0, 4) < 3).astype(jnp.int32), jax.random.fold_in(key_list[3], 1), 0, 1)
    return {"amplitudes": amplitudes, "integrals": integrals, "amplitude_mask": amplitude_mask, "integral_mask": integral_mask}


def mask_tiles(values, screen, row_tile, col_tile):
    height, breadth = values.shape
    tiled = values.reshape(height // row_tile, row_tile, breadth // col_tile, col_tile)
    tiled = tiled * screen.astype(values.dtype)[:, None, :, None]
    return tiled.reshape(height, breadth)


def reference(amplitudes, integrals, amplitude_mask, integral_mask):
    amp_masked = mask_tiles(amplitudes, amplitude_mask, OTILE, TILE)
    int_masked = mask_tiles(integrals, integral_mask, TILE, TILE)
    row_blocks = amp_masked.reshape(N_BLK, OP // N_BLK, CD)

    def block_product(block_rows):
        return (0.5 * jnp.dot(block_rows, int_masked, preferred_element_type=jnp.float32)).astype(jnp.bfloat16)

    return lax.map(block_product, row_blocks).reshape(OP, AB)
```

```python
import jax
import jax.numpy as jnp
from jax import lax
from jax.experimental import pallas as pl
from jax.experimental.pallas import tpu as pltpu
from jax.sharding import PartitionSpec as P

TILE = 128
OTILE = 16
NCH = 4
MESH = pl.DeviceIdType.MESH

OWN, B, F, Z, ZB, ZF, O, ZO = range(8)


def kernel(amps, ints, amask, imask, out, panels, rows, amp_in, int_in, load_sem,
           recv_x, recv_p, send_i, recv_a, send_a):
    depth, width = ints.shape
    height, _ = amps.shape
    chunk = depth // NCH
    blk, grp = lax.axis_index("blk"), lax.axis_index("grp")
    core, zl, x = lax.rem(blk, 2), lax.rem(blk // 2, 2), blk // 4
    y, zh = lax.rem(grp, 4), grp // 4

    def ring(i, step):
        return lax.rem(i + step + 4, 4)

    def kinds(c):
        d = 1 - 2 * c
        xb, xf, xo = ring(x, -d), ring(x, d), ring(x, 2)
        cells = [(x, zl), (xb, zl), (xf, zl), (x, 1 - zl), (xb, 1 - zl), (xf, 1 - zl),
                 (xo, zl), (xo, 1 - zl)]
        return [i * 4 + j * 2 + c for i, j in cells]

    mine, theirs = kinds(core), kinds(1 - core)
    d = 1 - 2 * core
    dev_xf, dev_xb = (mine[F], grp), (mine[B], grp)
    dev_z, dev_p = (mine[Z], grp), (theirs[OWN], grp)
    zcol = [zh, ring(zh, -d), ring(zh, d), ring(zh, 2)]
    yb, yf, yo = ring(y, -d), ring(y, d), ring(y, 2)
    dev_zf, dev_zb = (blk, zcol[2] * 4 + y), (blk, zcol[1] * 4 + y)
    dev_yf, dev_yb = (blk, zh * 4 + yf), (blk, zh * 4 + yb)

    barrier = pltpu.get_barrier_semaphore()
    everyone = (dev_zf, dev_zb, dev_yf, dev_yb, dev_z, dev_xf, dev_xb, dev_p)
    for dev in everyone:
        pl.semaphore_signal(barrier, inc=1, device_id=dev, device_id_type=MESH)

    load_a = pltpu.make_async_copy(amps, amp_in, load_sem.at[0])
    load_i = pltpu.make_async_copy(ints, int_in, load_sem.at[1])
    load_a.start()
    load_i.start()

    def arow(owner):
        return pl.ds(pl.multiple_of(owner * height, OTILE), height)

    load_a.wait()
    for r in range(height // OTILE):
        for k in range(depth // TILE):
            keep = jnp.full((OTILE, TILE), amask[r, k].astype(jnp.float32)).astype(jnp.bfloat16)
            tile = amp_in[r * OTILE:(r + 1) * OTILE, k * TILE:(k + 1) * TILE] * keep
            rows[pl.ds(pl.multiple_of(grp * height + r * OTILE, OTILE), OTILE),
                 k * TILE:(k + 1) * TILE] = tile
    load_i.wait()
    for k in range(depth // TILE):
        for j in range(width // TILE):
            keep = jnp.full((TILE, TILE), imask[k, j].astype(jnp.float32)).astype(jnp.bfloat16)
            tile = int_in[k * TILE:(k + 1) * TILE, j * TILE:(j + 1) * TILE] * keep
            panels[blk, k * TILE:(k + 1) * TILE, j * TILE:(j + 1) * TILE] = tile

    pl.semaphore_wait(barrier, len(everyone))

    routes = [(OWN, dev_xf, B), (OWN, dev_xb, F), (OWN, dev_z, Z), (B, dev_xf, O),
              (Z, dev_xf, ZB), (Z, dev_xb, ZF), (O, dev_z, ZO)]

    def panel_copy(n, k):
        kind, dev, there = routes[n]
        ref = panels.at[mine[kind], pl.ds(k * chunk, chunk)]
        return pltpu.make_async_remote_copy(
            src_ref=ref, dst_ref=ref, send_sem=send_i.at[n], recv_sem=recv_x.at[there - 1, k],
            device_id=dev, device_id_type=MESH)

    def pair_copy(kind, k):
        ref = panels.at[mine[kind], pl.ds(k * chunk, chunk)]
        return pltpu.make_async_remote_copy(
            src_ref=ref, dst_ref=ref, send_sem=send_i.at[7 + kind], recv_sem=recv_p.at[kind, k],
            device_id=dev_p, device_id_type=MESH)

    def arrived(kind, k):
        ref = panels.at[mine[kind], pl.ds(k * chunk, chunk)]
        pltpu.make_async_remote_copy(
            src_ref=ref, dst_ref=ref, send_sem=send_i.at[0], recv_sem=recv_x.at[kind - 1, k],
            device_id=dev_p, device_id_type=MESH).wait_recv()

    def relay(kind, k):
        arrived(kind, k)
        for n, route in enumerate(routes):
            if route[0] == kind:
                panel_copy(n, k).start()
        pair_copy(kind, k).start()

    def pair_arrived(kind):
        for k in range(NCH):
            ref = panels.at[theirs[kind], pl.ds(k * chunk, chunk)]
            pltpu.make_async_remote_copy(
                src_ref=ref, dst_ref=ref, send_sem=send_i.at[0], recv_sem=recv_p.at[kind, k],
                device_id=dev_p, device_id_type=MESH).wait_recv()

    def amp_copy(n, owner, dev, there):
        ref = rows.at[arow(owner)]
        return pltpu.make_async_remote_copy(
            src_ref=ref, dst_ref=ref, send_sem=send_a.at[n], recv_sem=recv_a.at[there],
            device_id=dev, device_id_type=MESH)

    def amp_arrived(there, owner):
        amp_copy(0, owner, dev_p, there).wait_recv()

    column = [zcol[j] * 4 + y for j in range(4)]
    behind = [zcol[j] * 4 + yb for j in range(4)]
    ahead = [zcol[j] * 4 + yf for j in range(4)]
    across = [zcol[j] * 4 + yo for j in range(4)]
    amp_sends = [amp_copy(0, grp, dev_zf, 0), amp_copy(1, grp, dev_zb, 1),
                 amp_copy(2, column[1], dev_zf, 2)]
    amp_sends += [amp_copy(3 + j, column[j], dev_yf, 3 + j) for j in range(4)]
    amp_sends += [amp_copy(7 + j, column[j], dev_yb, 7 + j) for j in range(4)]
    amp_sends += [amp_copy(11 + j, behind[j], dev_yf, 11 + j) for j in range(4)]

    def amp_column(j):
        if j:
            amp_arrived(j - 1, column[j])
        if j == 1:
            amp_sends[2].start()
        amp_sends[3 + j].start()
        amp_sends[7 + j].start()

    def amp_behind(j):
        amp_arrived(3 + j, behind[j])
        amp_sends[11 + j].start()

    def compute(panel):
        @pl.loop(0, rows.shape[0] // 256)
        def _(i):
            r = pl.ds(pl.multiple_of(i * 256, 256), 256)
            total = jnp.dot(rows[r, :], panels[panel], preferred_element_type=jnp.float32)
            out[r, pl.ds(pl.multiple_of(panel * width, width), width)] = (0.5 * total).astype(out.dtype)

    amp_sends[0].start()
    amp_sends[1].start()
    amp_column(0)
    for k in range(NCH):
        for n in range(3):
            panel_copy(n, k).start()
        pair_copy(OWN, k).start()

    amp_behind(0)
    relay(B, 0)
    amp_column(1)
    amp_column(2)
    relay(F, 0)
    relay(B, 1)
    relay(F, 1)
    amp_column(3)
    relay(Z, 0)
    amp_behind(1)
    relay(B, 2)
    amp_behind(2)
    relay(F, 2)
    relay(Z, 1)
    relay(B, 3)
    relay(F, 3)
    amp_behind(3)
    relay(Z, 2)
    relay(O, 0)
    relay(Z, 3)
    relay(O, 1)
    for j in range(4):
        amp_arrived(7 + j, ahead[j])
    relay(ZB, 0)
    relay(ZF, 0)
    for j in range(4):
        amp_arrived(11 + j, across[j])

    compute(mine[OWN])
    relay(O, 2)
    pair_arrived(OWN)
    compute(theirs[OWN])
    relay(O, 3)
    relay(ZB, 1)
    relay(ZF, 1)
    compute(mine[B])
    pair_arrived(B)
    relay(ZO, 0)
    compute(theirs[B])
    compute(mine[F])
    relay(ZB, 2)
    relay(ZF, 2)
    pair_arrived(F)
    compute(theirs[F])
    relay(ZO, 1)
    compute(mine[Z])
    pair_arrived(Z)
    relay(ZB, 3)
    relay(ZF, 3)
    compute(theirs[Z])
    relay(ZO, 2)
    compute(mine[O])
    pair_arrived(O)
    compute(theirs[O])
    relay(ZO, 3)
    for kind in (ZB, ZF):
        compute(mine[kind])
        pair_arrived(kind)
        compute(theirs[kind])
    compute(mine[ZO])
    pair_arrived(ZO)
    compute(theirs[ZO])

    for send in amp_sends:
        send.wait_send()
    for n in range(15):
        ref = panels.at[0]
        pltpu.make_async_remote_copy(
            src_ref=ref, dst_ref=ref, send_sem=send_i.at[n], recv_sem=recv_x.at[0, 0],
            device_id=dev_p, device_id_type=MESH).wait_send()


def local(amplitudes, integrals, amplitude_mask, integral_mask):
    height, depth = amplitudes.shape
    width = integrals.shape[1]
    n_blk, n_grp = lax.axis_size("blk"), lax.axis_size("grp")
    return pl.pallas_call(
        kernel,
        out_shape=jax.ShapeDtypeStruct((n_grp * height, n_blk * width), jnp.bfloat16),
        in_specs=[pl.BlockSpec(memory_space=pl.ANY)] * 2
        + [pl.BlockSpec(memory_space=pltpu.SMEM)] * 2,
        out_specs=pl.BlockSpec(memory_space=pltpu.VMEM),
        scratch_shapes=[
            pltpu.VMEM((n_blk, depth, width), jnp.bfloat16),
            pltpu.VMEM((n_grp * height, depth), jnp.bfloat16),
            pltpu.VMEM((height, depth), jnp.bfloat16),
            pltpu.VMEM((depth, width), jnp.bfloat16),
            pltpu.SemaphoreType.DMA((2,)),
            pltpu.SemaphoreType.DMA((7, NCH)),
            pltpu.SemaphoreType.DMA((8, NCH)),
            pltpu.SemaphoreType.DMA((15,)),
            pltpu.SemaphoreType.DMA((15,)),
            pltpu.SemaphoreType.DMA((15,)),
        ],
        compiler_params=pltpu.CompilerParams(
            collective_id=0, has_side_effects=True, vmem_limit_bytes=24 << 20),
        name="ladder",
    )(amplitudes, integrals, amplitude_mask, integral_mask)


def solution(mesh):
    return jax.shard_map(
        local,
        mesh=mesh,
        in_specs=(
            P(("blk", "grp"), None),
            P(None, ("grp", "blk")),
            P(("blk", "grp"), None),
            P(None, ("grp", "blk")),
        ),
        out_specs=P("blk", "grp"),
        check_vma=False,
    )
```

```python
import jax
import jax.numpy as jnp
from jax import lax
from jax.experimental import pallas as pl
from jax.experimental.pallas import tpu as pltpu
from jax.sharding import PartitionSpec as P

TILE = 128
OTILE = 16
NCH = 4
MESH = pl.DeviceIdType.MESH

OWN, B, F, Z, ZB, ZF, O, ZO = range(8)


ORDER = (
    "S0", "b0", "B0", "F0", "a1", "S1", "S2", "S3", "a2", "B1", "F1", "B2",
    "F2", "a3", "b1", "b2", "B3", "F3", "Z0", "Z1", "O0", "b3", "O1", "Z2",
    "O2", "Z3", "rows", "c.OWN", "p.OWN", "c.B", "p.B", "c.F", "p.F", "O3", "ZB0", "ZF0",
    "c.Z", "p.Z", "ZB1", "ZF1", "ZO0", "c.O", "ZB2", "ZF2", "ZO1", "ZO2", "ZB3", "ZF3",
    "ZO3", "p.O", "c.ZB", "p.ZB?", "p.ZF?", "p.ZO?",
)
LATE = (
    "c.ZF", "c.ZO", "p.ZB", "p.ZF", "p.ZO",
)
DONE = tuple(t for t in ORDER if "." in t and "?" not in t)
KINDS = dict(OWN=OWN, B=B, F=F, Z=Z, ZB=ZB, ZF=ZF, O=O, ZO=ZO)


def ring(i, step):
    return lax.rem(i + step + 4, 4)


def kinds(blk):
    core, zl, x = lax.rem(blk, 2), lax.rem(blk // 2, 2), blk // 4

    def of(c):
        d = 1 - 2 * c
        xb, xf, xo = ring(x, -d), ring(x, d), ring(x, 2)
        cells = [(x, zl), (xb, zl), (xf, zl), (x, 1 - zl), (xb, 1 - zl), (xf, 1 - zl),
                 (xo, zl), (xo, 1 - zl)]
        return [i * 4 + j * 2 + c for i, j in cells]

    return of(core), of(1 - core)


def panel_of(name, sides):
    return sides[name[0] == "p"][KINDS[name[2:]]]


def product(rows, panel):
    total = jnp.dot(rows[...], panel[...], preferred_element_type=jnp.float32)
    return (0.5 * total).astype(jnp.bfloat16)


def gather(amps, ints, amask_in, imask_in, done, panels, rows, amp_in, int_in, amask, imask,
           load_sem, recv_x, recv_p, send_i, recv_a, send_a):
    depth, width = ints.shape
    height, _ = amps.shape
    chunk = depth // NCH
    blk, grp = lax.axis_index("blk"), lax.axis_index("grp")
    core = lax.rem(blk, 2)
    y, zh = lax.rem(grp, 4), grp // 4

    mine, theirs = kinds(blk)
    d = 1 - 2 * core
    dev_xf, dev_xb = (mine[F], grp), (mine[B], grp)
    dev_z, dev_p = (mine[Z], grp), (theirs[OWN], grp)
    zcol = [zh, ring(zh, -d), ring(zh, d), ring(zh, 2)]
    yb, yf, yo = ring(y, -d), ring(y, d), ring(y, 2)
    dev_zf, dev_zb = (blk, zcol[2] * 4 + y), (blk, zcol[1] * 4 + y)
    dev_yf, dev_yb = (blk, zh * 4 + yf), (blk, zh * 4 + yb)

    barrier = pltpu.get_barrier_semaphore()
    everyone = (dev_zf, dev_zb, dev_yf, dev_yb, dev_z, dev_xf, dev_xb, dev_p)
    for dev in everyone:
        pl.semaphore_signal(barrier, inc=1, device_id=dev, device_id_type=MESH)

    loads = [pltpu.make_async_copy(*pair, load_sem.at[n]) for n, pair in enumerate(
        [(amask_in, amask), (imask_in, imask), (amps, amp_in), (ints, int_in)])]
    for load in loads:
        load.start()

    def arow(owner):
        return pl.ds(pl.multiple_of(owner * height, OTILE), height)

    loads[0].wait()
    loads[2].wait()
    for r in range(height // OTILE):
        for k in range(depth // TILE):
            keep = jnp.full((OTILE, TILE), amask[r, k].astype(jnp.float32)).astype(jnp.bfloat16)
            tile = amp_in[r * OTILE:(r + 1) * OTILE, k * TILE:(k + 1) * TILE] * keep
            rows[pl.ds(pl.multiple_of(grp * height + r * OTILE, OTILE), OTILE),
                 k * TILE:(k + 1) * TILE] = tile
    loads[1].wait()
    loads[3].wait()
    for k in range(depth // TILE):
        for j in range(width // TILE):
            keep = jnp.full((TILE, TILE), imask[j, k].astype(jnp.float32)).astype(jnp.bfloat16)
            tile = int_in[k * TILE:(k + 1) * TILE, j * TILE:(j + 1) * TILE] * keep
            panels[blk, k * TILE:(k + 1) * TILE, j * TILE:(j + 1) * TILE] = tile

    pl.semaphore_wait(barrier, len(everyone))

    routes = [(OWN, dev_xf, B), (OWN, dev_xb, F), (OWN, dev_z, Z), (B, dev_xf, O),
              (Z, dev_xf, ZB), (Z, dev_xb, ZF), (O, dev_z, ZO)]

    def panel_copy(n, k):
        kind, dev, there = routes[n]
        ref = panels.at[mine[kind], pl.ds(k * chunk, chunk)]
        return pltpu.make_async_remote_copy(
            src_ref=ref, dst_ref=ref, send_sem=send_i.at[n], recv_sem=recv_x.at[there - 1, k],
            device_id=dev, device_id_type=MESH)

    def pair_copy(kind, k):
        ref = panels.at[mine[kind], pl.ds(k * chunk, chunk)]
        return pltpu.make_async_remote_copy(
            src_ref=ref, dst_ref=ref, send_sem=send_i.at[7 + kind], recv_sem=recv_p.at[kind, k],
            device_id=dev_p, device_id_type=MESH)

    def arrived(kind, k):
        ref = panels.at[mine[kind], pl.ds(k * chunk, chunk)]
        pltpu.make_async_remote_copy(
            src_ref=ref, dst_ref=ref, send_sem=send_i.at[0], recv_sem=recv_x.at[kind - 1, k],
            device_id=dev_p, device_id_type=MESH).wait_recv()

    def relay(kind, k):
        arrived(kind, k)
        for n, route in enumerate(routes):
            if route[0] == kind:
                panel_copy(n, k).start()
        pair_copy(kind, k).start()

    def pair_arrived(kind):
        for k in range(NCH):
            ref = panels.at[theirs[kind], pl.ds(k * chunk, chunk)]
            pltpu.make_async_remote_copy(
                src_ref=ref, dst_ref=ref, send_sem=send_i.at[0], recv_sem=recv_p.at[kind, k],
                device_id=dev_p, device_id_type=MESH).wait_recv()

    def amp_copy(n, owner, dev, there):
        ref = rows.at[arow(owner)]
        return pltpu.make_async_remote_copy(
            src_ref=ref, dst_ref=ref, send_sem=send_a.at[n], recv_sem=recv_a.at[there],
            device_id=dev, device_id_type=MESH)

    def amp_arrived(there, owner):
        amp_copy(0, owner, dev_p, there).wait_recv()

    column = [zcol[j] * 4 + y for j in range(4)]
    behind = [zcol[j] * 4 + yb for j in range(4)]
    ahead = [zcol[j] * 4 + yf for j in range(4)]
    across = [zcol[j] * 4 + yo for j in range(4)]
    amp_sends = [amp_copy(0, grp, dev_zf, 0), amp_copy(1, grp, dev_zb, 1),
                 amp_copy(2, column[1], dev_zf, 2)]
    amp_sends += [amp_copy(3 + j, column[j], dev_yf, 3 + j) for j in range(4)]
    amp_sends += [amp_copy(7 + j, column[j], dev_yb, 7 + j) for j in range(4)]
    amp_sends += [amp_copy(11 + j, behind[j], dev_yf, 11 + j) for j in range(4)]

    def amp_column(j):
        if j:
            amp_arrived(j - 1, column[j])
        if j == 1:
            amp_sends[2].start()
        amp_sends[3 + j].start()
        amp_sends[7 + j].start()

    def amp_behind(j):
        amp_arrived(3 + j, behind[j])
        amp_sends[11 + j].start()

    amp_sends[0].start()
    amp_sends[1].start()
    amp_column(0)
    for k in range(NCH):
        panel_copy(0, k).start()
        panel_copy(1, k).start()
        pair_copy(OWN, k).start()

    for step in ORDER:
        if "." in step:
            if step[0] == "p":
                pair_arrived(KINDS[step[2:].rstrip("?")])
            if step in DONE:
                done[DONE.index(step)] = product(rows, panels.at[panel_of(step, (mine, theirs))])
        elif step == "rows":
            for j in range(4):
                amp_arrived(7 + j, ahead[j])
            for j in range(4):
                amp_arrived(11 + j, across[j])
        elif step[0] == "a":
            amp_column(int(step[1]))
        elif step[0] == "S":
            panel_copy(2, int(step[1])).start()
        elif step[0] == "b":
            amp_behind(int(step[1]))
        else:
            relay(KINDS[step[:-1]], int(step[-1]))

    for send in amp_sends:
        send.wait_send()
    for n in range(15):
        ref = panels.at[0]
        pltpu.make_async_remote_copy(
            src_ref=ref, dst_ref=ref, send_sem=send_i.at[n], recv_sem=recv_x.at[0, 0],
            device_id=dev_p, device_id_type=MESH).wait_send()


def finish(done, panels, rows, out, late, sems):
    sides = kinds(lax.axis_index("blk"))
    width = panels.shape[2]

    def write(name, block, n):
        start = pl.multiple_of(panel_of(name, sides) * width, width)
        return pltpu.make_async_copy(block, out.at[:, pl.ds(start, width)], sems.at[n])

    copies = [write(name, done.at[n], n) for n, name in enumerate(DONE)]
    for copy in copies:
        copy.start()
    for n, name in enumerate(LATE):
        late[n] = product(rows, panels.at[panel_of(name, sides)])
        copies.append(write(name, late.at[n], len(DONE) + n))
        copies[-1].start()
    for copy in copies:
        copy.wait()


def local(amplitudes, integrals, amplitude_mask, integral_mask):
    height, depth = amplitudes.shape
    width = integrals.shape[1]
    n_blk, n_grp = lax.axis_size("blk"), lax.axis_size("grp")
    vmem, hbm = pl.BlockSpec(memory_space=pltpu.VMEM), pl.BlockSpec(memory_space=pltpu.HBM)
    done, panels, rows = pl.pallas_call(
        gather,
        out_shape=[
            jax.ShapeDtypeStruct((len(DONE), n_grp * height, width), jnp.bfloat16),
            jax.ShapeDtypeStruct((n_blk, depth, width), jnp.bfloat16),
            jax.ShapeDtypeStruct((n_grp * height, depth), jnp.bfloat16),
        ],
        in_specs=[hbm] * 4,
        out_specs=[vmem] * 3,
        scratch_shapes=[
            pltpu.VMEM((height, depth), jnp.bfloat16),
            pltpu.VMEM((depth, width), jnp.bfloat16),
            pltpu.SMEM(amplitude_mask.shape, jnp.int32),
            pltpu.SMEM(integral_mask.shape[::-1], jnp.int32),
            pltpu.SemaphoreType.DMA((4,)),
            pltpu.SemaphoreType.DMA((7, NCH)),
            pltpu.SemaphoreType.DMA((8, NCH)),
            pltpu.SemaphoreType.DMA((15,)),
            pltpu.SemaphoreType.DMA((15,)),
            pltpu.SemaphoreType.DMA((15,)),
        ],
        compiler_params=pltpu.CompilerParams(
            collective_id=0, has_side_effects=True, vmem_limit_bytes=24 << 20),
        name="gather",
    )(*[pltpu.with_memory_space_constraint(v, pltpu.HBM)
        for v in (amplitudes, integrals, amplitude_mask, integral_mask.T)])
    return pl.pallas_call(
        finish,
        out_shape=jax.ShapeDtypeStruct((n_grp * height, n_blk * width), jnp.bfloat16),
        in_specs=[vmem] * 3,
        out_specs=hbm,
        scratch_shapes=[
            pltpu.VMEM((len(LATE), n_grp * height, width), jnp.bfloat16),
            pltpu.SemaphoreType.DMA((len(DONE) + len(LATE),)),
        ],
        compiler_params=pltpu.CompilerParams(vmem_limit_bytes=24 << 20),
        name="finish",
    )(done, panels, rows)


def solution(mesh):
    return jax.shard_map(
        local,
        mesh=mesh,
        in_specs=(
            P(("blk", "grp"), None),
            P(None, ("grp", "blk")),
            P(("blk", "grp"), None),
            P(None, ("grp", "blk")),
        ),
        out_specs=P("blk", "grp"),
        check_vma=False,
    )
```

```python
import jax
import jax.numpy as jnp
from jax import lax
from jax.experimental import pallas as pl
from jax.experimental.pallas import tpu as pltpu
from jax.sharding import PartitionSpec as P

TILE = 128
OTILE = 16
NCH = 4
MESH = pl.DeviceIdType.MESH

OWN, B, F, Z, ZB, ZF, O, ZO = range(8)


LOW = (
    "H-", "a0", "S0", "S1", "B0", "F0", "H+", "S2", "b0", "B1", "F1", "a1",
    "S3", "B2", "F2", "a2", "b1", "B3", "F3", "Z0", "b2", "Z1", "O0", "a3",
    "O1", "Z2", "O2", "Z3", "b3", "O3", "rows", "p.OWN?", "p.B?", "p.F?", "p.Z?", "c.OWN",
    "p.OWN", "c.B", "p.B", "c.F", "p.F", "c.Z", "p.Z", "c.O", "ZB0", "ZF0", "ZB1", "ZF1",
    "ZO0", "ZB2", "ZF2", "ZO1", "ZO2", "ZB3", "ZF3", "ZO3", "p.O?", "p.O", "c.ZB", "p.ZB?",
    "p.ZF?", "p.ZO?",
)
HIGH = (
    "H-", "a0", "S0", "H+", "b0", "B0", "F0", "a1", "S1", "S2", "S3", "a2",
    "B1", "F1", "B2", "F2", "a3", "b1", "b2", "B3", "F3", "Z0", "Z1", "O0",
    "b3", "O1", "Z2", "O2", "Z3", "O3", "rows", "p.OWN?", "p.B?", "p.F?", "p.Z?", "c.OWN",
    "p.OWN", "c.B", "p.B", "c.F", "p.F", "c.Z", "p.Z", "c.O", "ZB0", "ZF0", "ZB1", "ZF1",
    "ZO0", "ZB2", "ZF2", "ZO1", "ZO2", "ZB3", "ZF3", "ZO3", "p.O?", "p.O", "c.ZB", "p.ZB?",
    "p.ZF?", "p.ZO?",
)
LATE = (
    "c.ZF", "c.ZO", "p.ZB", "p.ZF", "p.ZO",
)
DONE = tuple(t for t in LOW if "." in t and "?" not in t)
KINDS = dict(OWN=OWN, B=B, F=F, Z=Z, ZB=ZB, ZF=ZF, O=O, ZO=ZO)


def ring(i, step):
    return lax.rem(i + step + 4, 4)


def kinds(blk):
    core, zl, x = lax.rem(blk, 2), lax.rem(blk // 2, 2), blk // 4

    def of(c):
        d = 1 - 2 * c
        xb, xf, xo = ring(x, -d), ring(x, d), ring(x, 2)
        cells = [(x, zl), (xb, zl), (xf, zl), (x, 1 - zl), (xb, 1 - zl), (xf, 1 - zl),
                 (xo, zl), (xo, 1 - zl)]
        return [i * 4 + j * 2 + c for i, j in cells]

    return of(core), of(1 - core)


def panel_of(name, sides):
    return sides[name[0] == "p"][KINDS[name[2:]]]


def product(rows, panel):
    total = jnp.dot(rows[...], panel[...], preferred_element_type=jnp.float32)
    return (0.5 * total).astype(jnp.bfloat16)


def gather(amps, ints, amask_in, imask_in, done, panels, rows, amp_in, int_in, amask, imask,
           load_sem, recv_x, recv_p, send_i, recv_a, send_a, answer):
    depth, width = ints.shape
    height, _ = amps.shape
    chunk = depth // NCH
    blk, grp = lax.axis_index("blk"), lax.axis_index("grp")
    core = lax.rem(blk, 2)
    y, zh = lax.rem(grp, 4), grp // 4

    mine, theirs = kinds(blk)
    d = 1 - 2 * core
    dev_xf, dev_xb = (mine[F], grp), (mine[B], grp)
    dev_z, dev_p = (mine[Z], grp), (theirs[OWN], grp)
    zcol = [zh, ring(zh, -d), ring(zh, d), ring(zh, 2)]
    yb, yf, yo = ring(y, -d), ring(y, d), ring(y, 2)
    dev_zf, dev_zb = (blk, zcol[2] * 4 + y), (blk, zcol[1] * 4 + y)
    dev_yf, dev_yb = (blk, zh * 4 + yf), (blk, zh * 4 + yb)

    barrier = pltpu.get_barrier_semaphore()
    near = (dev_yf, dev_yb, dev_z, dev_xf, dev_xb, dev_p)
    for dev in near:
        pl.semaphore_signal(barrier, inc=1, device_id=dev, device_id_type=MESH)
    column_devs = ((zcol[2], dev_zf), (zcol[1], dev_zb))
    for other, dev in column_devs:
        @pl.when(other > zh)
        def _(dev=dev):
            pl.semaphore_signal(barrier, inc=1, device_id=dev, device_id_type=MESH)

    loads = [pltpu.make_async_copy(*pair, load_sem.at[n]) for n, pair in enumerate(
        [(amask_in, amask), (imask_in, imask), (amps, amp_in), (ints, int_in)])]
    for load in loads:
        load.start()

    def arow(owner):
        return pl.ds(pl.multiple_of(owner * height, OTILE), height)

    loads[0].wait()
    loads[2].wait()
    for r in range(height // OTILE):
        for k in range(depth // TILE):
            keep = jnp.full((OTILE, TILE), amask[r, k].astype(jnp.float32)).astype(jnp.bfloat16)
            tile = amp_in[r * OTILE:(r + 1) * OTILE, k * TILE:(k + 1) * TILE] * keep
            rows[pl.ds(pl.multiple_of(grp * height + r * OTILE, OTILE), OTILE),
                 k * TILE:(k + 1) * TILE] = tile
    loads[1].wait()
    loads[3].wait()
    for k in range(depth // TILE):
        for j in range(width // TILE):
            keep = jnp.full((TILE, TILE), imask[j, k].astype(jnp.float32)).astype(jnp.bfloat16)
            tile = int_in[k * TILE:(k + 1) * TILE, j * TILE:(j + 1) * TILE] * keep
            panels[blk, k * TILE:(k + 1) * TILE, j * TILE:(j + 1) * TILE] = tile

    pl.semaphore_wait(barrier, len(near) + (zh + 1) // 2)
    for n, (other, dev) in enumerate(column_devs):
        @pl.when(other < zh)
        def _(n=n, dev=dev):
            pl.semaphore_signal(answer.at[1 - n], inc=1, device_id=dev, device_id_type=MESH)

    routes = [(OWN, dev_xf, B), (OWN, dev_xb, F), (OWN, dev_z, Z), (B, dev_xf, O),
              (Z, dev_xf, ZB), (Z, dev_xb, ZF), (O, dev_z, ZO)]

    def panel_copy(n, k):
        kind, dev, there = routes[n]
        ref = panels.at[mine[kind], pl.ds(k * chunk, chunk)]
        return pltpu.make_async_remote_copy(
            src_ref=ref, dst_ref=ref, send_sem=send_i.at[n], recv_sem=recv_x.at[there - 1, k],
            device_id=dev, device_id_type=MESH)

    def pair_copy(kind, k):
        ref = panels.at[mine[kind], pl.ds(k * chunk, chunk)]
        return pltpu.make_async_remote_copy(
            src_ref=ref, dst_ref=ref, send_sem=send_i.at[7 + kind], recv_sem=recv_p.at[kind, k],
            device_id=dev_p, device_id_type=MESH)

    def arrived(kind, k):
        ref = panels.at[mine[kind], pl.ds(k * chunk, chunk)]
        pltpu.make_async_remote_copy(
            src_ref=ref, dst_ref=ref, send_sem=send_i.at[0], recv_sem=recv_x.at[kind - 1, k],
            device_id=dev_p, device_id_type=MESH).wait_recv()

    def relay(kind, k):
        arrived(kind, k)
        for n, route in enumerate(routes):
            if route[0] == kind:
                panel_copy(n, k).start()
        pair_copy(kind, k).start()

    def pair_arrived(kind):
        for k in range(NCH):
            ref = panels.at[theirs[kind], pl.ds(k * chunk, chunk)]
            pltpu.make_async_remote_copy(
                src_ref=ref, dst_ref=ref, send_sem=send_i.at[0], recv_sem=recv_p.at[kind, k],
                device_id=dev_p, device_id_type=MESH).wait_recv()

    def amp_copy(n, owner, dev, there):
        ref = rows.at[arow(owner)]
        return pltpu.make_async_remote_copy(
            src_ref=ref, dst_ref=ref, send_sem=send_a.at[n], recv_sem=recv_a.at[there],
            device_id=dev, device_id_type=MESH)

    def amp_arrived(there, owner):
        amp_copy(0, owner, dev_p, there).wait_recv()

    column = [zcol[j] * 4 + y for j in range(4)]
    behind = [zcol[j] * 4 + yb for j in range(4)]
    ahead = [zcol[j] * 4 + yf for j in range(4)]
    across = [zcol[j] * 4 + yo for j in range(4)]
    amp_sends = [amp_copy(0, grp, dev_zf, 0), amp_copy(1, grp, dev_zb, 1),
                 amp_copy(2, column[1], dev_zf, 2)]
    amp_sends += [amp_copy(3 + j, column[j], dev_yf, 3 + j) for j in range(4)]
    amp_sends += [amp_copy(7 + j, column[j], dev_yb, 7 + j) for j in range(4)]
    amp_sends += [amp_copy(11 + j, behind[j], dev_yf, 11 + j) for j in range(4)]

    def amp_column(j):
        if j:
            amp_arrived(j - 1, column[j])
        if j == 1:
            amp_sends[2].start()
        amp_sends[3 + j].start()
        amp_sends[7 + j].start()

    def amp_behind(j):
        amp_arrived(3 + j, behind[j])
        amp_sends[11 + j].start()

    def amp_own(upper):
        for n, (other, _) in enumerate(column_devs):
            @pl.when(other > zh if upper else other < zh)
            def _(n=n):
                if upper:
                    pl.semaphore_wait(answer.at[n], 1)
                amp_sends[n].start()

    for k in range(NCH):
        panel_copy(0, k).start()
        panel_copy(1, k).start()
        pair_copy(OWN, k).start()

    def run(order):
        for step in order:
            if "." in step:
                if step[-1] == "?":
                    pair_arrived(KINDS[step[2:-1]])
                else:
                    done[DONE.index(step)] = product(rows, panels.at[panel_of(step, (mine, theirs))])
            elif step in ("H-", "H+"):
                amp_own(step == "H+")
            elif step == "rows":
                for j in range(4):
                    amp_arrived(7 + j, ahead[j])
                for j in range(4):
                    amp_arrived(11 + j, across[j])
            elif step[0] == "a":
                amp_column(int(step[1]))
            elif step[0] == "S":
                panel_copy(2, int(step[1])).start()
            elif step[0] == "b":
                amp_behind(int(step[1]))
            else:
                relay(KINDS[step[:-1]], int(step[-1]))

    @pl.when(zh < 2)
    def _():
        run(LOW)

    @pl.when(zh >= 2)
    def _():
        run(HIGH)

    for send in amp_sends:
        send.wait_send()
    for n in range(15):
        ref = panels.at[0]
        pltpu.make_async_remote_copy(
            src_ref=ref, dst_ref=ref, send_sem=send_i.at[n], recv_sem=recv_x.at[0, 0],
            device_id=dev_p, device_id_type=MESH).wait_send()


def finish(done, panels, rows, out, late, sems):
    sides = kinds(lax.axis_index("blk"))
    width = panels.shape[2]

    def write(name, block, n):
        start = pl.multiple_of(panel_of(name, sides) * width, width)
        return pltpu.make_async_copy(block, out.at[:, pl.ds(start, width)], sems.at[n])

    copies = [write(name, done.at[n], n) for n, name in enumerate(DONE)]
    for copy in copies:
        copy.start()
    for n, name in enumerate(LATE):
        late[n] = product(rows, panels.at[panel_of(name, sides)])
        copies.append(write(name, late.at[n], len(DONE) + n))
        copies[-1].start()
    for copy in copies:
        copy.wait()


def local(amplitudes, integrals, amplitude_mask, integral_mask):
    height, depth = amplitudes.shape
    width = integrals.shape[1]
    n_blk, n_grp = lax.axis_size("blk"), lax.axis_size("grp")
    vmem, hbm = pl.BlockSpec(memory_space=pltpu.VMEM), pl.BlockSpec(memory_space=pltpu.HBM)
    done, panels, rows = pl.pallas_call(
        gather,
        out_shape=[
            jax.ShapeDtypeStruct((len(DONE), n_grp * height, width), jnp.bfloat16),
            jax.ShapeDtypeStruct((n_blk, depth, width), jnp.bfloat16),
            jax.ShapeDtypeStruct((n_grp * height, depth), jnp.bfloat16),
        ],
        in_specs=[hbm] * 4,
        out_specs=[vmem] * 3,
        scratch_shapes=[
            pltpu.VMEM((height, depth), jnp.bfloat16),
            pltpu.VMEM((depth, width), jnp.bfloat16),
            pltpu.SMEM(amplitude_mask.shape, jnp.int32),
            pltpu.SMEM(integral_mask.shape[::-1], jnp.int32),
            pltpu.SemaphoreType.DMA((4,)),
            pltpu.SemaphoreType.DMA((7, NCH)),
            pltpu.SemaphoreType.DMA((8, NCH)),
            pltpu.SemaphoreType.DMA((15,)),
            pltpu.SemaphoreType.DMA((15,)),
            pltpu.SemaphoreType.DMA((15,)),
            pltpu.SemaphoreType.REGULAR((2,)),
        ],
        compiler_params=pltpu.CompilerParams(
            collective_id=0, has_side_effects=True, vmem_limit_bytes=24 << 20),
        name="gather",
    )(*[pltpu.with_memory_space_constraint(v, pltpu.HBM)
        for v in (amplitudes, integrals, amplitude_mask, integral_mask.T)])
    return pl.pallas_call(
        finish,
        out_shape=jax.ShapeDtypeStruct((n_grp * height, n_blk * width), jnp.bfloat16),
        in_specs=[vmem] * 3,
        out_specs=hbm,
        scratch_shapes=[
            pltpu.VMEM((len(LATE), n_grp * height, width), jnp.bfloat16),
            pltpu.SemaphoreType.DMA((len(DONE) + len(LATE),)),
        ],
        compiler_params=pltpu.CompilerParams(vmem_limit_bytes=24 << 20),
        name="finish",
    )(done, panels, rows)


def solution(mesh):
    return jax.shard_map(
        local,
        mesh=mesh,
        in_specs=(
            P(("blk", "grp"), None),
            P(None, ("grp", "blk")),
            P(("blk", "grp"), None),
            P(None, ("grp", "blk")),
        ),
        out_specs=P("blk", "grp"),
        check_vma=False,
    )
```

```python
import jax
import jax.numpy as jnp
from jax import lax
from jax.experimental import pallas as pl
from jax.experimental.pallas import tpu as pltpu
from jax.sharding import PartitionSpec as P

TILE = 128
OTILE = 16
NCH = 4
MESH = pl.DeviceIdType.MESH

OWN, B, F, Z, ZB, ZF, O, ZO = range(8)


LOW = (
    "H-", "a0", "S0", "S1", "B0", "F0", "H+", "S2", "b0", "B1", "F1", "a1",
    "S3", "B2", "F2", "a2", "b1", "B3", "F3", "b2", "Z0", "a3", "Z1", "O0",
    "O1", "Z2", "O2", "b3", "Z3", "O3", "rows", "p.OWN?", "p.B?", "p.F?", "p.Z?", "c.OWN",
    "p.OWN", "c.B", "p.B", "c.F", "p.F", "c.Z", "p.Z", "c.O", "ZB0", "ZF0", "ZB1", "ZF1",
    "ZO0", "ZB2", "ZF2", "ZO1", "ZO2", "ZB3", "ZF3", "ZO3", "p.O?", "p.O", "c.ZB", "p.ZB?",
    "p.ZF?", "p.ZO?",
)
HIGH = (
    "H-", "a0", "S0", "H+", "b0", "B0", "F0", "a1", "S1", "S2", "S3", "a2",
    "B1", "F1", "B2", "F2", "a3", "b1", "b2", "B3", "F3", "Z0", "Z1", "O0",
    "b3", "O1", "Z2", "O2", "Z3", "O3", "rows", "p.OWN?", "p.B?", "p.F?", "p.Z?", "c.OWN",
    "p.OWN", "c.B", "p.B", "c.F", "p.F", "c.Z", "p.Z", "c.O", "ZB0", "ZF0", "ZB1", "ZF1",
    "ZO0", "ZB2", "ZF2", "ZO1", "ZO2", "ZB3", "ZF3", "ZO3", "p.O?", "p.O", "c.ZB", "p.ZB?",
    "p.ZF?", "p.ZO?",
)
LATE = (
    "c.ZF", "c.ZO", "p.ZB", "p.ZF", "p.ZO",
)
DONE = tuple(t for t in LOW if "." in t and "?" not in t)
KINDS = dict(OWN=OWN, B=B, F=F, Z=Z, ZB=ZB, ZF=ZF, O=O, ZO=ZO)


def ring(i, step):
    return lax.rem(i + step + 4, 4)


def kinds(blk):
    core, zl, x = lax.rem(blk, 2), lax.rem(blk // 2, 2), blk // 4

    def of(c):
        d = 1 - 2 * c
        xb, xf, xo = ring(x, -d), ring(x, d), ring(x, 2)
        cells = [(x, zl), (xb, zl), (xf, zl), (x, 1 - zl), (xb, 1 - zl), (xf, 1 - zl),
                 (xo, zl), (xo, 1 - zl)]
        return [i * 4 + j * 2 + c for i, j in cells]

    return of(core), of(1 - core)


def panel_of(name, sides):
    return sides[name[0] == "p"][KINDS[name[2:]]]


def product(rows, panel):
    total = jnp.dot(rows[...], panel[...], preferred_element_type=jnp.float32)
    return (0.5 * total).astype(jnp.bfloat16)


def gather(amps, ints, amask_in, imask_in, done, panels, rows, amp_in, int_in, amask, imask,
           load_sem, recv_x, recv_p, send_i, recv_a, send_a, answer):
    depth, width = ints.shape
    height, _ = amps.shape
    chunk = depth // NCH
    blk, grp = lax.axis_index("blk"), lax.axis_index("grp")
    core = lax.rem(blk, 2)
    y, zh = lax.rem(grp, 4), grp // 4

    mine, theirs = kinds(blk)
    d = 1 - 2 * core
    dev_xf, dev_xb = (mine[F], grp), (mine[B], grp)
    dev_z, dev_p = (mine[Z], grp), (theirs[OWN], grp)
    zcol = [zh, ring(zh, -d), ring(zh, d), ring(zh, 2)]
    yb, yf, yo = ring(y, -d), ring(y, d), ring(y, 2)
    dev_zf, dev_zb = (blk, zcol[2] * 4 + y), (blk, zcol[1] * 4 + y)
    dev_yf, dev_yb = (blk, zh * 4 + yf), (blk, zh * 4 + yb)

    barrier = pltpu.get_barrier_semaphore()
    near = (dev_yf, dev_yb, dev_z, dev_xf, dev_xb, dev_p)
    for dev in near:
        pl.semaphore_signal(barrier, inc=1, device_id=dev, device_id_type=MESH)
    def answers(other):
        return jnp.logical_and(other < zh, zh + other != 5)

    def waits(other):
        return jnp.logical_and(other > zh, zh + other != 5)

    column_devs = ((zcol[2], dev_zf), (zcol[1], dev_zb))
    for other, dev in column_devs:
        @pl.when(jnp.logical_not(answers(other)))
        def _(dev=dev):
            pl.semaphore_signal(barrier, inc=1, device_id=dev, device_id_type=MESH)

    loads = [pltpu.make_async_copy(*pair, load_sem.at[n]) for n, pair in enumerate(
        [(amask_in, amask), (imask_in, imask), (amps, amp_in), (ints, int_in)])]
    for load in loads:
        load.start()

    def arow(owner):
        return pl.ds(pl.multiple_of(owner * height, OTILE), height)

    loads[0].wait()
    loads[2].wait()
    for r in range(height // OTILE):
        for k in range(depth // TILE):
            keep = jnp.full((OTILE, TILE), amask[r, k].astype(jnp.float32)).astype(jnp.bfloat16)
            tile = amp_in[r * OTILE:(r + 1) * OTILE, k * TILE:(k + 1) * TILE] * keep
            rows[pl.ds(pl.multiple_of(grp * height + r * OTILE, OTILE), OTILE),
                 k * TILE:(k + 1) * TILE] = tile
    loads[1].wait()
    loads[3].wait()
    for k in range(depth // TILE):
        for j in range(width // TILE):
            keep = jnp.full((TILE, TILE), imask[j, k].astype(jnp.float32)).astype(jnp.bfloat16)
            tile = int_in[k * TILE:(k + 1) * TILE, j * TILE:(j + 1) * TILE] * keep
            panels[blk, k * TILE:(k + 1) * TILE, j * TILE:(j + 1) * TILE] = tile

    pl.semaphore_wait(barrier, len(near) + jnp.minimum(zh, 2))
    for n, (other, dev) in enumerate(column_devs):
        @pl.when(answers(other))
        def _(n=n, dev=dev):
            pl.semaphore_signal(answer.at[1 - n], inc=1, device_id=dev, device_id_type=MESH)

    routes = [(OWN, dev_xf, B), (OWN, dev_xb, F), (OWN, dev_z, Z), (B, dev_xf, O),
              (Z, dev_xf, ZB), (Z, dev_xb, ZF), (O, dev_z, ZO)]

    def panel_copy(n, k):
        kind, dev, there = routes[n]
        ref = panels.at[mine[kind], pl.ds(k * chunk, chunk)]
        return pltpu.make_async_remote_copy(
            src_ref=ref, dst_ref=ref, send_sem=send_i.at[n], recv_sem=recv_x.at[there - 1, k],
            device_id=dev, device_id_type=MESH)

    def pair_copy(kind, k):
        ref = panels.at[mine[kind], pl.ds(k * chunk, chunk)]
        return pltpu.make_async_remote_copy(
            src_ref=ref, dst_ref=ref, send_sem=send_i.at[7 + kind], recv_sem=recv_p.at[kind, k],
            device_id=dev_p, device_id_type=MESH)

    def arrived(kind, k):
        ref = panels.at[mine[kind], pl.ds(k * chunk, chunk)]
        pltpu.make_async_remote_copy(
            src_ref=ref, dst_ref=ref, send_sem=send_i.at[0], recv_sem=recv_x.at[kind - 1, k],
            device_id=dev_p, device_id_type=MESH).wait_recv()

    def relay(kind, k):
        arrived(kind, k)
        for n, route in enumerate(routes):
            if route[0] == kind:
                panel_copy(n, k).start()
        pair_copy(kind, k).start()

    def pair_arrived(kind):
        for k in range(NCH):
            ref = panels.at[theirs[kind], pl.ds(k * chunk, chunk)]
            pltpu.make_async_remote_copy(
                src_ref=ref, dst_ref=ref, send_sem=send_i.at[0], recv_sem=recv_p.at[kind, k],
                device_id=dev_p, device_id_type=MESH).wait_recv()

    def amp_copy(n, owner, dev, there):
        ref = rows.at[arow(owner)]
        return pltpu.make_async_remote_copy(
            src_ref=ref, dst_ref=ref, send_sem=send_a.at[n], recv_sem=recv_a.at[there],
            device_id=dev, device_id_type=MESH)

    def amp_arrived(there, owner):
        amp_copy(0, owner, dev_p, there).wait_recv()

    column = [zcol[j] * 4 + y for j in range(4)]
    behind = [zcol[j] * 4 + yb for j in range(4)]
    ahead = [zcol[j] * 4 + yf for j in range(4)]
    across = [zcol[j] * 4 + yo for j in range(4)]
    amp_sends = [amp_copy(0, grp, dev_zf, 0), amp_copy(1, grp, dev_zb, 1),
                 amp_copy(2, column[1], dev_zf, 2)]
    amp_sends += [amp_copy(3 + j, column[j], dev_yf, 3 + j) for j in range(4)]
    amp_sends += [amp_copy(7 + j, column[j], dev_yb, 7 + j) for j in range(4)]
    amp_sends += [amp_copy(11 + j, behind[j], dev_yf, 11 + j) for j in range(4)]

    def amp_column(j):
        if j:
            amp_arrived(j - 1, column[j])
        if j == 1:
            amp_sends[2].start()
        amp_sends[3 + j].start()
        amp_sends[7 + j].start()

    def amp_behind(j):
        amp_arrived(3 + j, behind[j])
        amp_sends[11 + j].start()

    def amp_own(upper):
        for n, (other, _) in enumerate(column_devs):
            @pl.when(waits(other) if upper else jnp.logical_not(waits(other)))
            def _(n=n):
                if upper:
                    pl.semaphore_wait(answer.at[n], 1)
                amp_sends[n].start()

    for k in range(NCH):
        panel_copy(0, k).start()
        panel_copy(1, k).start()
        pair_copy(OWN, k).start()

    def run(order):
        for step in order:
            if "." in step:
                if step[-1] == "?":
                    pair_arrived(KINDS[step[2:-1]])
                else:
                    done[DONE.index(step)] = product(rows, panels.at[panel_of(step, (mine, theirs))])
            elif step in ("H-", "H+"):
                amp_own(step == "H+")
            elif step == "rows":
                for j in range(4):
                    amp_arrived(7 + j, ahead[j])
                for j in range(4):
                    amp_arrived(11 + j, across[j])
            elif step[0] == "a":
                amp_column(int(step[1]))
            elif step[0] == "S":
                panel_copy(2, int(step[1])).start()
            elif step[0] == "b":
                amp_behind(int(step[1]))
            else:
                relay(KINDS[step[:-1]], int(step[-1]))

    @pl.when(zh < 2)
    def _():
        run(LOW)

    @pl.when(zh >= 2)
    def _():
        run(HIGH)

    for send in amp_sends:
        send.wait_send()
    for n in range(15):
        ref = panels.at[0]
        pltpu.make_async_remote_copy(
            src_ref=ref, dst_ref=ref, send_sem=send_i.at[n], recv_sem=recv_x.at[0, 0],
            device_id=dev_p, device_id_type=MESH).wait_send()


def finish(done, panels, rows, out, late, sems):
    sides = kinds(lax.axis_index("blk"))
    width = panels.shape[2]

    def write(name, block, n):
        start = pl.multiple_of(panel_of(name, sides) * width, width)
        return pltpu.make_async_copy(block, out.at[:, pl.ds(start, width)], sems.at[n])

    copies = [write(name, done.at[n], n) for n, name in enumerate(DONE)]
    for copy in copies:
        copy.start()
    for n, name in enumerate(LATE):
        late[n] = product(rows, panels.at[panel_of(name, sides)])
        copies.append(write(name, late.at[n], len(DONE) + n))
        copies[-1].start()
    for copy in copies:
        copy.wait()


def local(amplitudes, integrals, amplitude_mask, integral_mask):
    height, depth = amplitudes.shape
    width = integrals.shape[1]
    n_blk, n_grp = lax.axis_size("blk"), lax.axis_size("grp")
    vmem, hbm = pl.BlockSpec(memory_space=pltpu.VMEM), pl.BlockSpec(memory_space=pltpu.HBM)
    done, panels, rows = pl.pallas_call(
        gather,
        out_shape=[
            jax.ShapeDtypeStruct((len(DONE), n_grp * height, width), jnp.bfloat16),
            jax.ShapeDtypeStruct((n_blk, depth, width), jnp.bfloat16),
            jax.ShapeDtypeStruct((n_grp * height, depth), jnp.bfloat16),
        ],
        in_specs=[hbm] * 4,
        out_specs=[vmem] * 3,
        scratch_shapes=[
            pltpu.VMEM((height, depth), jnp.bfloat16),
            pltpu.VMEM((depth, width), jnp.bfloat16),
            pltpu.SMEM(amplitude_mask.shape, jnp.int32),
            pltpu.SMEM(integral_mask.shape[::-1], jnp.int32),
            pltpu.SemaphoreType.DMA((4,)),
            pltpu.SemaphoreType.DMA((7, NCH)),
            pltpu.SemaphoreType.DMA((8, NCH)),
            pltpu.SemaphoreType.DMA((15,)),
            pltpu.SemaphoreType.DMA((15,)),
            pltpu.SemaphoreType.DMA((15,)),
            pltpu.SemaphoreType.REGULAR((2,)),
        ],
        compiler_params=pltpu.CompilerParams(
            collective_id=0, has_side_effects=True, vmem_limit_bytes=24 << 20),
        name="gather",
    )(*[pltpu.with_memory_space_constraint(v, pltpu.HBM)
        for v in (amplitudes, integrals, amplitude_mask, integral_mask.T)])
    return pl.pallas_call(
        finish,
        out_shape=jax.ShapeDtypeStruct((n_grp * height, n_blk * width), jnp.bfloat16),
        in_specs=[vmem] * 3,
        out_specs=hbm,
        scratch_shapes=[
            pltpu.VMEM((len(LATE), n_grp * height, width), jnp.bfloat16),
            pltpu.SemaphoreType.DMA((len(DONE) + len(LATE),)),
        ],
        compiler_params=pltpu.CompilerParams(vmem_limit_bytes=24 << 20),
        name="finish",
    )(done, panels, rows)


def solution(mesh):
    return jax.shard_map(
        local,
        mesh=mesh,
        in_specs=(
            P(("blk", "grp"), None),
            P(None, ("grp", "blk")),
            P(("blk", "grp"), None),
            P(None, ("grp", "blk")),
        ),
        out_specs=P("blk", "grp"),
        check_vma=False,
    )
```

```python
import jax
import jax.numpy as jnp
from jax import lax
from jax.experimental import pallas as pl
from jax.experimental.pallas import tpu as pltpu
from jax.sharding import PartitionSpec as P

TILE = 128
OTILE = 16
NCH = 4
MESH = pl.DeviceIdType.MESH

OWN, B, F, Z, ZB, ZF, O, ZO = range(8)


LOW = (
    "H-", "a0", "S0", "S1", "B0", "F0", "H+", "S2", "b0", "B1", "F1", "a1",
    "S3", "B2", "F2", "a2", "b1", "B3", "F3", "b2", "Z0", "a3", "Z1", "O0",
    "O1", "Z2", "O2", "b3", "Z3", "O3", "rows", "p.OWN?", "p.B?", "p.F?", "p.Z?", "p.O?",
    "c.OWN", "p.OWN", "c.B", "p.B", "c.F", "p.F", "c.Z", "p.Z", "c.O", "p.O", "ZB0", "ZF0",
    "ZB1", "ZF1", "ZO0", "ZB2", "ZF2", "ZO1", "ZO2", "ZB3", "ZF3", "ZO3", "c.ZB", "p.ZB?",
    "p.ZF?", "p.ZO?",
)
HIGH = (
    "H-", "a0", "S0", "H+", "b0", "B0", "F0", "a1", "S1", "S2", "S3", "a2",
    "B1", "F1", "B2", "F2", "a3", "b1", "b2", "B3", "F3", "Z0", "Z1", "O0",
    "b3", "O1", "Z2", "O2", "Z3", "O3", "rows", "p.OWN?", "p.B?", "p.F?", "p.Z?", "p.O?",
    "c.OWN", "p.OWN", "c.B", "p.B", "c.F", "p.F", "c.Z", "p.Z", "c.O", "p.O", "ZB0", "ZF0",
    "ZB1", "ZF1", "ZO0", "ZB2", "ZF2", "ZO1", "ZO2", "ZB3", "ZF3", "ZO3", "c.ZB", "p.ZB?",
    "p.ZF?", "p.ZO?",
)
LATE = (
    "c.ZF", "c.ZO", "p.ZB", "p.ZF", "p.ZO",
)
DONE = tuple(t for t in LOW if "." in t and "?" not in t)
KINDS = dict(OWN=OWN, B=B, F=F, Z=Z, ZB=ZB, ZF=ZF, O=O, ZO=ZO)


def ring(i, step):
    return lax.rem(i + step + 4, 4)


def kinds(blk):
    core, zl, x = lax.rem(blk, 2), lax.rem(blk // 2, 2), blk // 4

    def of(c):
        d = 1 - 2 * c
        xb, xf, xo = ring(x, -d), ring(x, d), ring(x, 2)
        cells = [(x, zl), (xb, zl), (xf, zl), (x, 1 - zl), (xb, 1 - zl), (xf, 1 - zl),
                 (xo, zl), (xo, 1 - zl)]
        return [i * 4 + j * 2 + c for i, j in cells]

    return of(core), of(1 - core)


def panel_of(name, sides):
    return sides[name[0] == "p"][KINDS[name[2:]]]


def product(rows, panel):
    total = jnp.dot(rows[...], panel[...], preferred_element_type=jnp.float32)
    return (0.5 * total).astype(jnp.bfloat16)


def gather(amps, ints, amask_in, imask_in, done, panels, rows, amp_in, int_in, amask, imask,
           load_sem, recv_x, recv_p, send_i, recv_a, send_a, answer):
    depth, width = ints.shape
    height, _ = amps.shape
    chunk = depth // NCH
    blk, grp = lax.axis_index("blk"), lax.axis_index("grp")
    core = lax.rem(blk, 2)
    y, zh = lax.rem(grp, 4), grp // 4

    mine, theirs = kinds(blk)
    d = 1 - 2 * core
    dev_xf, dev_xb = (mine[F], grp), (mine[B], grp)
    dev_z, dev_p = (mine[Z], grp), (theirs[OWN], grp)
    zcol = [zh, ring(zh, -d), ring(zh, d), ring(zh, 2)]
    yb, yf, yo = ring(y, -d), ring(y, d), ring(y, 2)
    dev_zf, dev_zb = (blk, zcol[2] * 4 + y), (blk, zcol[1] * 4 + y)
    dev_yf, dev_yb = (blk, zh * 4 + yf), (blk, zh * 4 + yb)

    barrier = pltpu.get_barrier_semaphore()
    near = (dev_yf, dev_yb, dev_z, dev_xf, dev_xb, dev_p)
    for dev in near:
        pl.semaphore_signal(barrier, inc=1, device_id=dev, device_id_type=MESH)
    def answers(other):
        return jnp.logical_and(other < zh, zh + other != 5)

    def waits(other):
        return jnp.logical_and(other > zh, zh + other != 5)

    column_devs = ((zcol[2], dev_zf), (zcol[1], dev_zb))
    for other, dev in column_devs:
        @pl.when(jnp.logical_not(answers(other)))
        def _(dev=dev):
            pl.semaphore_signal(barrier, inc=1, device_id=dev, device_id_type=MESH)

    loads = [pltpu.make_async_copy(*pair, load_sem.at[n]) for n, pair in enumerate(
        [(amask_in, amask), (imask_in, imask), (amps, amp_in), (ints, int_in)])]
    for load in loads:
        load.start()

    def arow(owner):
        return pl.ds(pl.multiple_of(owner * height, OTILE), height)

    loads[0].wait()
    loads[2].wait()
    for r in range(height // OTILE):
        for k in range(depth // TILE):
            keep = jnp.full((OTILE, TILE), amask[r, k].astype(jnp.float32)).astype(jnp.bfloat16)
            tile = amp_in[r * OTILE:(r + 1) * OTILE, k * TILE:(k + 1) * TILE] * keep
            rows[pl.ds(pl.multiple_of(grp * height + r * OTILE, OTILE), OTILE),
                 k * TILE:(k + 1) * TILE] = tile
    loads[1].wait()
    loads[3].wait()
    for k in range(depth // TILE):
        for j in range(width // TILE):
            keep = jnp.full((TILE, TILE), imask[j, k].astype(jnp.float32)).astype(jnp.bfloat16)
            tile = int_in[k * TILE:(k + 1) * TILE, j * TILE:(j + 1) * TILE] * keep
            panels[blk, k * TILE:(k + 1) * TILE, j * TILE:(j + 1) * TILE] = tile

    pl.semaphore_wait(barrier, len(near) + jnp.minimum(zh, 2))
    for n, (other, dev) in enumerate(column_devs):
        @pl.when(answers(other))
        def _(n=n, dev=dev):
            pl.semaphore_signal(answer.at[1 - n], inc=1, device_id=dev, device_id_type=MESH)

    routes = [(OWN, dev_xf, B), (OWN, dev_xb, F), (OWN, dev_z, Z), (B, dev_xf, O),
              (Z, dev_xf, ZB), (Z, dev_xb, ZF), (O, dev_z, ZO)]

    def panel_copy(n, k):
        kind, dev, there = routes[n]
        ref = panels.at[mine[kind], pl.ds(k * chunk, chunk)]
        return pltpu.make_async_remote_copy(
            src_ref=ref, dst_ref=ref, send_sem=send_i.at[n], recv_sem=recv_x.at[there - 1, k],
            device_id=dev, device_id_type=MESH)

    def pair_copy(kind, k):
        ref = panels.at[mine[kind], pl.ds(k * chunk, chunk)]
        return pltpu.make_async_remote_copy(
            src_ref=ref, dst_ref=ref, send_sem=send_i.at[7 + kind], recv_sem=recv_p.at[kind, k],
            device_id=dev_p, device_id_type=MESH)

    def arrived(kind, k):
        ref = panels.at[mine[kind], pl.ds(k * chunk, chunk)]
        pltpu.make_async_remote_copy(
            src_ref=ref, dst_ref=ref, send_sem=send_i.at[0], recv_sem=recv_x.at[kind - 1, k],
            device_id=dev_p, device_id_type=MESH).wait_recv()

    def relay(kind, k):
        arrived(kind, k)
        for n, route in enumerate(routes):
            if route[0] == kind:
                panel_copy(n, k).start()
        pair_copy(kind, k).start()

    def pair_arrived(kind):
        for k in range(NCH):
            ref = panels.at[theirs[kind], pl.ds(k * chunk, chunk)]
            pltpu.make_async_remote_copy(
                src_ref=ref, dst_ref=ref, send_sem=send_i.at[0], recv_sem=recv_p.at[kind, k],
                device_id=dev_p, device_id_type=MESH).wait_recv()

    def amp_copy(n, owner, dev, there):
        ref = rows.at[arow(owner)]
        return pltpu.make_async_remote_copy(
            src_ref=ref, dst_ref=ref, send_sem=send_a.at[n], recv_sem=recv_a.at[there],
            device_id=dev, device_id_type=MESH)

    def amp_arrived(there, owner):
        amp_copy(0, owner, dev_p, there).wait_recv()

    column = [zcol[j] * 4 + y for j in range(4)]
    behind = [zcol[j] * 4 + yb for j in range(4)]
    ahead = [zcol[j] * 4 + yf for j in range(4)]
    across = [zcol[j] * 4 + yo for j in range(4)]
    amp_sends = [amp_copy(0, grp, dev_zf, 0), amp_copy(1, grp, dev_zb, 1),
                 amp_copy(2, column[1], dev_zf, 2)]
    amp_sends += [amp_copy(3 + j, column[j], dev_yf, 3 + j) for j in range(4)]
    amp_sends += [amp_copy(7 + j, column[j], dev_yb, 7 + j) for j in range(4)]
    amp_sends += [amp_copy(11 + j, behind[j], dev_yf, 11 + j) for j in range(4)]

    def amp_column(j):
        if j:
            amp_arrived(j - 1, column[j])
        if j == 1:
            amp_sends[2].start()
        amp_sends[3 + j].start()
        amp_sends[7 + j].start()

    def amp_behind(j):
        amp_arrived(3 + j, behind[j])
        amp_sends[11 + j].start()

    def amp_own(upper):
        for n, (other, _) in enumerate(column_devs):
            @pl.when(waits(other) if upper else jnp.logical_not(waits(other)))
            def _(n=n):
                if upper:
                    pl.semaphore_wait(answer.at[n], 1)
                amp_sends[n].start()

    for k in range(NCH):
        panel_copy(0, k).start()
        panel_copy(1, k).start()
        pair_copy(OWN, k).start()

    def run(order):
        for step in order:
            if "." in step:
                if step[-1] == "?":
                    pair_arrived(KINDS[step[2:-1]])
                else:
                    done[DONE.index(step)] = product(rows, panels.at[panel_of(step, (mine, theirs))])
            elif step in ("H-", "H+"):
                amp_own(step == "H+")
            elif step == "rows":
                for j in range(4):
                    amp_arrived(7 + j, ahead[j])
                for j in range(4):
                    amp_arrived(11 + j, across[j])
            elif step[0] == "a":
                amp_column(int(step[1]))
            elif step[0] == "S":
                panel_copy(2, int(step[1])).start()
            elif step[0] == "b":
                amp_behind(int(step[1]))
            else:
                relay(KINDS[step[:-1]], int(step[-1]))

    @pl.when(zh < 2)
    def _():
        run(LOW)

    @pl.when(zh >= 2)
    def _():
        run(HIGH)

    for send in amp_sends:
        send.wait_send()
    for n in range(15):
        ref = panels.at[0]
        pltpu.make_async_remote_copy(
            src_ref=ref, dst_ref=ref, send_sem=send_i.at[n], recv_sem=recv_x.at[0, 0],
            device_id=dev_p, device_id_type=MESH).wait_send()


def finish(done, panels, rows, out, late, sems):
    sides = kinds(lax.axis_index("blk"))
    width = panels.shape[2]

    def write(name, block, n):
        start = pl.multiple_of(panel_of(name, sides) * width, width)
        return pltpu.make_async_copy(block, out.at[:, pl.ds(start, width)], sems.at[n])

    copies = [write(name, done.at[n], n) for n, name in enumerate(DONE)]
    for copy in copies:
        copy.start()
    for n, name in enumerate(LATE):
        late[n] = product(rows, panels.at[panel_of(name, sides)])
        copies.append(write(name, late.at[n], len(DONE) + n))
        copies[-1].start()
    for copy in copies:
        copy.wait()


def local(amplitudes, integrals, amplitude_mask, integral_mask):
    height, depth = amplitudes.shape
    width = integrals.shape[1]
    n_blk, n_grp = lax.axis_size("blk"), lax.axis_size("grp")
    vmem, hbm = pl.BlockSpec(memory_space=pltpu.VMEM), pl.BlockSpec(memory_space=pltpu.HBM)
    done, panels, rows = pl.pallas_call(
        gather,
        out_shape=[
            jax.ShapeDtypeStruct((len(DONE), n_grp * height, width), jnp.bfloat16),
            jax.ShapeDtypeStruct((n_blk, depth, width), jnp.bfloat16),
            jax.ShapeDtypeStruct((n_grp * height, depth), jnp.bfloat16),
        ],
        in_specs=[hbm] * 4,
        out_specs=[vmem] * 3,
        scratch_shapes=[
            pltpu.VMEM((height, depth), jnp.bfloat16),
            pltpu.VMEM((depth, width), jnp.bfloat16),
            pltpu.SMEM(amplitude_mask.shape, jnp.int32),
            pltpu.SMEM(integral_mask.shape[::-1], jnp.int32),
            pltpu.SemaphoreType.DMA((4,)),
            pltpu.SemaphoreType.DMA((7, NCH)),
            pltpu.SemaphoreType.DMA((8, NCH)),
            pltpu.SemaphoreType.DMA((15,)),
            pltpu.SemaphoreType.DMA((15,)),
            pltpu.SemaphoreType.DMA((15,)),
            pltpu.SemaphoreType.REGULAR((2,)),
        ],
        compiler_params=pltpu.CompilerParams(
            collective_id=0, has_side_effects=True, vmem_limit_bytes=24 << 20),
        name="gather",
    )(*[pltpu.with_memory_space_constraint(v, pltpu.HBM)
        for v in (amplitudes, integrals, amplitude_mask, integral_mask.T)])
    return pl.pallas_call(
        finish,
        out_shape=jax.ShapeDtypeStruct((n_grp * height, n_blk * width), jnp.bfloat16),
        in_specs=[vmem] * 3,
        out_specs=hbm,
        scratch_shapes=[
            pltpu.VMEM((len(LATE), n_grp * height, width), jnp.bfloat16),
            pltpu.SemaphoreType.DMA((len(DONE) + len(LATE),)),
        ],
        compiler_params=pltpu.CompilerParams(vmem_limit_bytes=24 << 20),
        name="finish",
    )(done, panels, rows)


def solution(mesh):
    return jax.shard_map(
        local,
        mesh=mesh,
        in_specs=(
            P(("blk", "grp"), None),
            P(None, ("grp", "blk")),
            P(("blk", "grp"), None),
            P(None, ("grp", "blk")),
        ),
        out_specs=P("blk", "grp"),
        check_vma=False,
    )
```
